32 devices in a mesh: seq: 8 (over y, x, core), tp: 4 (over z).
Axes of the slice: x: 2, y: 2, z: 4, core: 2. Of those that a mesh axis runs over, the one named last changes fastest.
Arguments:
- layer_input: bfloat16 [8192, 2048], P('seq', 'tp'), may hold values from -18 to 18
- gain_one: float32 [2048], P('tp'), may hold values from 0.25 to 1.75
- query_weight: bfloat16 [2048, 2048], P('seq', 'tp'), may hold values from -0.13258252 to 0.13258252
- key_weight: bfloat16 [2048, 2048], P('seq', 'tp'), may hold values from -0.13258252 to 0.13258252
- value_weight: bfloat16 [2048, 4096], P('seq', 'tp'), may hold values from -0.13258252 to 0.13258252
- gate_weight: bfloat16 [2048, 4096], P('seq', 'tp'), may hold values from -0.13258252 to 0.13258252
- out_weight: bfloat16 [4096, 2048], P('tp', 'seq'), may hold values from -0.13258252 to 0.13258252
- gain_two: float32 [2048], P('tp'), may hold values from 0.25 to 1.75
- up_weight: bfloat16 [2048, 4096], P(None, 'tp'), may hold values from -0.13258252 to 0.13258252
- down_weight: bfloat16 [4096, 2048], P('tp'), may hold values from -0.13258252 to 0.13258252
- cotangent: bfloat16 [8192, 2048], P('seq', 'tp'), may hold values from -6 to 6
Outputs:
- layer_output: bfloat16 [8192, 2048], P('seq', 'tp')
- input_grad: bfloat16 [8192, 2048], P('seq', 'tp')
- gain_one_grad: float32 [2048], P('tp')
- query_weight_grad: float32 [2048, 2048], P('seq', 'tp')
- key_weight_grad: float32 [2048, 2048], P('seq', 'tp')
- value_weight_grad: float32 [2048, 4096], P('seq', 'tp')
- gate_weight_grad: float32 [2048, 4096], P('seq', 'tp')
- out_weight_grad: float32 [4096, 2048], P('tp', 'seq')
- gain_two_grad: float32 [2048], P('tp')
- up_weight_grad: float32 [2048, 4096], P(None, 'tp')
- down_weight_grad: float32 [4096, 2048], P('tp')
The draws below stay inside these ranges and needn't reach their ends.
All inputs are finite; a program needn't handle non-finite values.
Results may differ from the reference program's by a relative error of at most 0.022.
Values may be sent and summed in bfloat16 or wider, within the bound.
No kernel may reach another device: no remote copies, remote signals or barrier semaphores. Data moves between devices by JAX's collectives and lax.ppermute only.
A program may use at most 192 MiB of HBM per device.

```python
import math
import jax
import jax.numpy as jnp
from jax import lax

D = 2048
HEADS = 8
KEY_DIM = 256
VAL_DIM = 512
FF = 4096
BLOCK = 512
TOKENS = 8192
SEQ_LEN = 8192
N_SEQ = 8


def drawn_field(key, shape, scale):
    base = jnp.clip(jax.random.normal(key, shape, jnp.float32), -6.0, 6.0)
    return base * scale


def draw_layer_input(key, part):
    base = drawn_field(jax.random.fold_in(key, 11), (TOKENS, D), 1.0)
    pairing = jax.random.permutation(jax.random.fold_in(key, 12), N_SEQ)
    row_block = jnp.arange(TOKENS) // (TOKENS // N_SEQ)
    col_block = jnp.arange(D) // (D // N_SEQ)
    chosen = pairing[row_block]
    boost = jnp.where(col_block[None, :] == chosen[:, None], 3.0, 1.0)
    return (base * boost).astype(jnp.bfloat16)


def draw_query_weight(key, part):
    return drawn_field(jax.random.fold_in(key, 21), (D, HEADS * KEY_DIM), D ** (-0.5)).astype(jnp.bfloat16)


def draw_key_weight(key, part):
    return drawn_field(jax.random.fold_in(key, 22), (D, HEADS * KEY_DIM), D ** (-0.5)).astype(jnp.bfloat16)


def draw_value_weight(key, part):
    return drawn_field(jax.random.fold_in(key, 23), (D, HEADS * VAL_DIM), D ** (-0.5)).astype(jnp.bfloat16)


def draw_gate_weight(key, part):
    return drawn_field(jax.random.fold_in(key, 24), (D, HEADS * VAL_DIM), D ** (-0.5)).astype(jnp.bfloat16)


def draw_out_weight(key, part):
    return drawn_field(jax.random.fold_in(key, 25), (HEADS * VAL_DIM, D), (HEADS * VAL_DIM // 2) ** (-0.5)).astype(jnp.bfloat16)


def draw_up_weight(key, part):
    return drawn_field(jax.random.fold_in(key, 26), (D, FF), D ** (-0.5)).astype(jnp.bfloat16)


def draw_down_weight(key, part):
    return drawn_field(jax.random.fold_in(key, 27), (FF, D), (FF // 2) ** (-0.5)).astype(jnp.bfloat16)


def draw_cotangent(key, part):
    return drawn_field(jax.random.fold_in(key, 28), (TOKENS, D), 1.0).astype(jnp.bfloat16)


def setup_inputs(seed: int = 0) -> dict:
    key_list = jax.random.split(jax.random.key(seed), 12)
    return {
        "layer_input": draw_layer_input(jax.random.fold_in(key_list[11], 71), 0),
        "gain_one": jnp.clip(1.0 + 0.15 * jax.random.normal(key_list[1], (D,), jnp.float32), 0.25, 1.75),
        "query_weight": draw_query_weight(jax.random.fold_in(key_list[11], 71), 0),
        "key_weight": draw_key_weight(jax.random.fold_in(key_list[11], 71), 0),
        "value_weight": draw_value_weight(jax.random.fold_in(key_list[11], 71), 0),
        "gate_weight": draw_gate_weight(jax.random.fold_in(key_list[11], 71), 0),
        "out_weight": draw_out_weight(jax.random.fold_in(key_list[11], 71), 0),
        "gain_two": jnp.clip(1.0 + 0.15 * jax.random.normal(key_list[7], (D,), jnp.float32), 0.25, 1.75),
        "up_weight": draw_up_weight(jax.random.fold_in(key_list[11], 71), 0),
        "down_weight": draw_down_weight(jax.random.fold_in(key_list[11], 71), 0),
        "cotangent": draw_cotangent(jax.random.fold_in(key_list[11], 71), 0),
    }


norm_eps = 1e-05
group_eps = 1.0
highest_precision_mode = lax.Precision.HIGHEST

@jax.custom_vjp
def low(v):
    return lax.optimization_barrier(v.astype(jnp.bfloat16)).astype(jnp.float32)

@jax.custom_vjp
def low_back(v):
    return v

def low_keep(v):
    return (low(v), None)

def low_pass(kept, grad):
    return (grad,)

def back_keep(v):
    return (v, None)

def back_low(kept, grad):
    return (low(grad),)
low.defvjp(low_keep, low_pass)
low_back.defvjp(back_keep, back_low)

def matmul(left, right):
    return jnp.dot(left, right, precision=highest_precision_mode)

def layer_norm(tensor, gain_part):
    average = lax.optimization_barrier(jnp.mean(tensor, axis=-1, keepdims=True))
    centered = tensor - average
    spread = lax.optimization_barrier(jnp.mean(centered * centered, axis=-1, keepdims=True))
    return centered * lax.rsqrt(spread + norm_eps) * gain_part

def rotary_tables(positions, halfway):
    frequency = jnp.exp(jnp.float32(-math.log(10000.0)) * jnp.arange(halfway, dtype=jnp.float32) / jnp.float32(halfway))
    angles = positions.astype(jnp.float32)[:, None] * frequency[None, :]
    return (jnp.cos(angles), jnp.sin(angles))

def rotate(tensor, cosine, sine_table):
    halfway = tensor.shape[-1] // 2
    former = tensor[..., :halfway]
    latter = tensor[..., halfway:]
    cos_part = cosine[:, None, :]
    sin_part = sine_table[:, None, :]
    return jnp.concatenate([former * cos_part - latter * sin_part, former * sin_part + latter * cos_part], axis=-1)

def decay_tables(log_gamma, block_len):
    offsets = jnp.arange(block_len, dtype=jnp.float32)
    lagged = offsets[:, None] - offsets[None, :]
    causal = (lagged >= 0.0).astype(jnp.float32)
    within = causal[None] * jnp.exp(jnp.maximum(lagged, 0.0)[None] * log_gamma[:, None, None])
    outward_result = jnp.exp((offsets + 1.0)[None, :] * log_gamma[:, None])
    inward = jnp.exp((jnp.float32(block_len - 1) - offsets)[None, :] * log_gamma[:, None])
    return (within, outward_result.T, inward.T)

def gate_mix(gate_raw, retained, head_count):
    grouped = retained.reshape(retained.shape[0], head_count, -1)
    centered = grouped - lax.optimization_barrier(jnp.mean(grouped, axis=-1, keepdims=True))
    normed = centered * lax.rsqrt(lax.optimization_barrier(jnp.mean(centered * centered, axis=-1, keepdims=True)) + group_eps)
    return jax.nn.silu(gate_raw) * normed.reshape(gate_raw.shape)

def retention(query_low, key_low, value_low):
    tok_count = query_low.shape[0]
    block_count = tok_count // BLOCK
    head_ids = jnp.arange(HEADS, dtype=jnp.float32)
    log_gamma = jnp.log(1.0 - jnp.exp2(-5.0 - head_ids))
    within, outward_result, inward = decay_tables(log_gamma, BLOCK)
    block_decay_factor = jnp.exp(jnp.float32(BLOCK) * log_gamma)[:, None, None]
    query_blocks = query_low.reshape(block_count, BLOCK, HEADS, KEY_DIM)
    key_blocks = key_low.reshape(block_count, BLOCK, HEADS, KEY_DIM)
    value_blocks = value_low.reshape(block_count, BLOCK, HEADS, VAL_DIM)
    block_starts = jnp.arange(block_count, dtype=jnp.int32) * jnp.int32(BLOCK)
    keeps = (block_starts % jnp.int32(SEQ_LEN) != 0).astype(jnp.float32)

    def advance(retention_state, inputs):
        query_slice, key_part, value_slice, keep_factor = inputs
        retention_state = keep_factor * retention_state
        scores = jnp.einsum('nhk,mhk->hnm', query_slice, key_part, precision=highest_precision_mode)
        weights = low(low_back(scores) * within)
        inside = jnp.einsum('hnm,mhv->nhv', weights, value_slice, precision=highest_precision_mode)
        carried_state_sum = outward_result[:, :, None] * jnp.einsum('xfy,fyp->xfp', query_slice, retention_state, precision=highest_precision_mode)
        key_value_outer = inward[:, :, None] * key_part
        retention_state = block_decay_factor * retention_state + jnp.einsum('qul,qui->uli', key_value_outer, value_slice, precision=highest_precision_mode)
        return (retention_state, low_back(inside + carried_state_sum))
    initial = jnp.zeros((HEADS, KEY_DIM, VAL_DIM), dtype=jnp.float32)
    _, outputs = lax.scan(jax.checkpoint(advance), initial, (query_blocks, key_blocks, value_blocks, keeps))
    return outputs.reshape(tok_count, HEADS * VAL_DIM)

def forward(x_float, gain_one, query_weight, key_weight, value_weight, gate_weight, out_weight, gain_two, up_weight, down_weight):
    tok_count = x_float.shape[0]
    positions = (jnp.arange(tok_count, dtype=jnp.int32) % jnp.int32(SEQ_LEN)).astype(jnp.int32)
    cosine, sine_table = rotary_tables(positions, KEY_DIM // 2)
    shared_one = low(layer_norm(x_float, gain_one))
    query_raw = low_back(matmul(shared_one, query_weight)).reshape(tok_count, HEADS, KEY_DIM)
    key_raw = low_back(matmul(shared_one, key_weight)).reshape(tok_count, HEADS, KEY_DIM)
    query_low = low(rotate(query_raw, cosine, sine_table))
    key_low = low(rotate(key_raw, cosine, sine_table) * jnp.float32(1.0 / math.sqrt(KEY_DIM)))
    value_low = low(low_back(matmul(shared_one, value_weight))).reshape(tok_count, HEADS, VAL_DIM)
    gate_raw = low_back(matmul(shared_one, gate_weight))
    retained = retention(query_low, key_low, value_low)
    mixed = low(gate_mix(gate_raw, retained, HEADS))
    hidden = x_float + low_back(matmul(mixed, out_weight))
    shared_two = low(layer_norm(hidden, gain_two))
    up_pre = low_back(matmul(shared_two, up_weight))
    activated = low(jax.nn.gelu(up_pre))
    return hidden + low_back(matmul(activated, down_weight))

def reference(layer_input, gain_one, query_weight, key_weight, value_weight, gate_weight, out_weight, gain_two, up_weight, down_weight, cotangent):
    floats = (layer_input.astype(jnp.float32), gain_one.astype(jnp.float32), query_weight.astype(jnp.float32), key_weight.astype(jnp.float32), value_weight.astype(jnp.float32), gate_weight.astype(jnp.float32), out_weight.astype(jnp.float32), gain_two.astype(jnp.float32), up_weight.astype(jnp.float32), down_weight.astype(jnp.float32))
    result, pull = jax.vjp(forward, *floats)
    grads = pull(cotangent.astype(jnp.float32))
    return (result.astype(jnp.bfloat16), grads[0].astype(jnp.bfloat16), grads[1], grads[2], grads[3], grads[4], grads[5], grads[6], grads[7], grads[8], grads[9])
```

```python
import functools
import math

import jax
import jax.numpy as jnp
from jax import lax
from jax.experimental import pallas as pl
from jax.experimental.pallas import tpu as pltpu
from jax.sharding import PartitionSpec as P

KEY_DIM = 256
VAL_DIM = 512
BLOCK = 512
MAXLEN = 8192
NORM_EPS = 1e-05
GROUP_EPS = 1.0
F32 = jnp.float32
BF16 = jnp.bfloat16
VMEM_LIMIT = 56 * 1024 * 1024


def dot(a, b, ca, cb):
    return lax.dot_general(a, b, (((ca,), (cb,)), ((), ())), preferred_element_type=F32)


def params(**kw):
    return pltpu.CompilerParams(vmem_limit_bytes=VMEM_LIMIT, **kw)


def cost(flops, nbytes):
    return pl.CostEstimate(flops=int(flops), bytes_accessed=int(nbytes), transcendentals=0)


def swap(a, bit, axis="seq"):
    n = lax.axis_size(axis)
    return lax.ppermute(a, axis, [(i, i ^ bit) for i in range(n)])


def outer_bits(flip):
    bits = [1 << k for k in range(1, (lax.axis_size("seq") - 1).bit_length())]
    return bits[::-1] if flip else bits


def xor_gather(a, flip):
    pieces = {0: a}
    for bit in outer_bits(flip) + [1]:
        for j in list(pieces):
            pieces[j ^ bit] = swap(pieces[j], bit)
    return pieces


def xor_finish(pieces, flip):
    for bit in outer_bits(flip)[::-1]:
        for j in sorted(pieces):
            if j & bit:
                got = swap(pieces.pop(j).astype(BF16), bit)
                pieces[j ^ bit] = pieces[j ^ bit] + got.astype(F32)
    return pieces[0]


def order_of(n):
    return [j for j in range(n) if j % 2 == 0] + [j for j in range(n) if j % 2 == 1]


def row_norm(x):
    mean = jnp.mean(x, axis=1, keepdims=True)
    c = x - mean
    r = lax.rsqrt(jnp.mean(c * c, axis=1, keepdims=True) + NORM_EPS)
    return c * r, r


def block_at(ids, j, size):
    return pl.ds(pl.multiple_of(lax.bitwise_xor(ids[0], jnp.int32(j)) * size, size), size)


def norm_one_kernel(order, ids, x_ref, gain_ref, o_ref, tmp):
    size = x_ref.shape[1] // len(order)
    n, _ = row_norm(x_ref[...].astype(F32))
    tmp[...] = (n * gain_ref[...]).astype(BF16)
    for p, j in enumerate(order):
        o_ref[:, p * size : (p + 1) * size] = tmp[:, block_at(ids, j, size)]


def norm_one(ids, x, gain, n_seq):
    rows, d = x.shape
    tile = 256
    return pl.pallas_call(
        functools.partial(norm_one_kernel, order_of(n_seq)),
        grid_spec=pltpu.PrefetchScalarGridSpec(
            num_scalar_prefetch=1,
            grid=(rows // tile,),
            in_specs=[
                pl.BlockSpec((tile, d), lambda i, ids: (i, 0)),
                pl.BlockSpec((1, d), lambda i, ids: (0, 0)),
            ],
            out_specs=pl.BlockSpec((tile, d), lambda i, ids: (i, 0)),
            scratch_shapes=[pltpu.VMEM((tile, d), BF16)],
        ),
        out_shape=jax.ShapeDtypeStruct((rows, d), BF16),
        compiler_params=params(),
        cost_estimate=cost(rows * d * 10, rows * d * 4),
        name="norm_one",
    )(ids, x, gain)


def norm_two_kernel(order, ids, r_ref, x_ref, gain_ref, h_ref, a_ref, b_ref):
    size = x_ref.shape[1] // len(order)
    for p, j in enumerate(order):
        at = block_at(ids, j, size)
        h_ref[:, at] = x_ref[:, at].astype(F32) + r_ref[:, p * size : (p + 1) * size].astype(F32)
    n, _ = row_norm(h_ref[...])
    out = (n * gain_ref[...]).astype(BF16)
    half = a_ref.shape[0]
    a_ref[...] = out[:half]
    b_ref[...] = out[half:]


def norm_two(ids, r, x, gain, n_seq):
    rows, d = r.shape
    half = rows // 2
    return pl.pallas_call(
        functools.partial(norm_two_kernel, order_of(n_seq)),
        grid_spec=pltpu.PrefetchScalarGridSpec(
            num_scalar_prefetch=1,
            grid=(1,),
            in_specs=[
                pl.BlockSpec((rows, d), lambda i, ids: (0, 0)),
                pl.BlockSpec((rows, d), lambda i, ids: (ids[1], 0)),
                pl.BlockSpec((1, d), lambda i, ids: (0, 0)),
            ],
            out_specs=[
                pl.BlockSpec((rows, d), lambda i, ids: (0, 0)),
                pl.BlockSpec((half, d), lambda i, ids: (0, 0)),
                pl.BlockSpec((half, d), lambda i, ids: (0, 0)),
            ],
        ),
        out_shape=[
            jax.ShapeDtypeStruct((rows, d), F32),
            jax.ShapeDtypeStruct((half, d), BF16),
            jax.ShapeDtypeStruct((half, d), BF16),
        ],
        compiler_params=params(),
        cost_estimate=cost(rows * d * 10, rows * d * 10),
        name="norm_two",
    )(ids, r, x, gain)


def norm_two_back_kernel(order, ids, ga_ref, gb_ref, h_ref, cot_ref, gain_ref, gh_ref, br_ref, gg_ref):
    size = h_ref.shape[1] // len(order)
    n, r = row_norm(h_ref[...])
    g = jnp.concatenate([ga_ref[...], gb_ref[...]], axis=0)
    gg_ref[...] = jnp.sum(g * n, axis=0, keepdims=True)
    e = g * gain_ref[...]
    back = r * (e - jnp.mean(e, axis=1, keepdims=True) - n * jnp.mean(e * n, axis=1, keepdims=True))
    gh_ref[...] = cot_ref[...].astype(F32) + back
    for p, j in enumerate(order):
        br_ref[:, p * size : (p + 1) * size] = gh_ref[:, block_at(ids, j, size)].astype(BF16)


def norm_two_back(ids, ga, gb, hidden, cot, gain, n_seq):
    rows, d = hidden.shape
    half = rows // 2
    whole = pl.BlockSpec((rows, d), lambda i, ids: (0, 0))
    part = pl.BlockSpec((half, d), lambda i, ids: (0, 0))
    line = pl.BlockSpec((1, d), lambda i, ids: (0, 0))
    return pl.pallas_call(
        functools.partial(norm_two_back_kernel, order_of(n_seq)),
        grid_spec=pltpu.PrefetchScalarGridSpec(
            num_scalar_prefetch=1,
            grid=(1,),
            in_specs=[part, part, whole, whole, line],
            out_specs=[whole, whole, line],
        ),
        out_shape=[
            jax.ShapeDtypeStruct((rows, d), F32),
            jax.ShapeDtypeStruct((rows, d), BF16),
            jax.ShapeDtypeStruct((1, d), F32),
        ],
        compiler_params=params(),
        cost_estimate=cost(rows * d * 20, rows * d * 16),
        name="norm_two_back",
    )(ids, ga, gb, hidden, cot, gain)


def norm_one_back_kernel(order, ids, g_ref, x_ref, gain_ref, gh_ref, o_ref, gg_ref, tmp):
    size = x_ref.shape[1] // len(order)
    i = pl.program_id(0)
    for p, j in enumerate(order):
        tmp[:, block_at(ids, j, size)] = g_ref[:, p * size : (p + 1) * size]
    n, r = row_norm(x_ref[...].astype(F32))
    g = tmp[...]
    part = jnp.sum(g * n, axis=0, keepdims=True)

    @pl.when(i == 0)
    def _():
        gg_ref[...] = part

    @pl.when(i > 0)
    def _():
        gg_ref[...] += part

    e = g * gain_ref[...]
    back = r * (e - jnp.mean(e, axis=1, keepdims=True) - n * jnp.mean(e * n, axis=1, keepdims=True))

    @pl.when(i == ids[1])
    def _():
        o_ref[...] = (back + gh_ref[...]).astype(BF16)

    @pl.when(i != ids[1])
    def _():
        o_ref[...] = back.astype(BF16)


def norm_one_back(ids, g, x, gain, grad_hidden, n_seq):
    rows, d = x.shape
    tile = grad_hidden.shape[0]
    step = pl.BlockSpec((tile, d), lambda i, ids: (i, 0))
    line = pl.BlockSpec((1, d), lambda i, ids: (0, 0))
    return pl.pallas_call(
        functools.partial(norm_one_back_kernel, order_of(n_seq)),
        grid_spec=pltpu.PrefetchScalarGridSpec(
            num_scalar_prefetch=1,
            grid=(rows // tile,),
            in_specs=[step, step, line, pl.BlockSpec((tile, d), lambda i, ids: (0, 0))],
            out_specs=[step, line],
            scratch_shapes=[pltpu.VMEM((tile, d), F32)],
        ),
        out_shape=[jax.ShapeDtypeStruct((rows, d), BF16), jax.ShapeDtypeStruct((1, d), F32)],
        compiler_params=params(),
        cost_estimate=cost(rows * d * 20, rows * d * 8),
        name="norm_one_back",
    )(ids, g, x, gain, grad_hidden)


def turn(v, c, s):
    h = v.shape[1] // 2
    a, b = v[:, :h], v[:, h:]
    return jnp.concatenate([a * c - b * s, a * s + b * c], axis=1)


def turn_back(v, c, s):
    h = v.shape[1] // 2
    a, b = v[:, :h], v[:, h:]
    return jnp.concatenate([a * c + b * s, b * c - a * s], axis=1)


def powers(lg, start, count, step):
    at = lax.broadcasted_iota(jnp.int32, (count, 1), 0).astype(F32)
    return jnp.exp((start + step * at) * lg)


def decay_within(lg, size):
    lag = lax.broadcasted_iota(jnp.int32, (size, size), 0) - lax.broadcasted_iota(
        jnp.int32, (size, size), 1
    )
    return jnp.where(lag >= 0, jnp.exp(jnp.maximum(lag, 0).astype(F32) * lg), 0.0)


def keys_kernel(lg_ref, q_ref, k_ref, v_ref, c_ref, s_ref, qo_ref, ko_ref, end_ref):
    lg = lg_ref[pl.program_id(0)]
    rows = q_ref.shape[0]
    c, s = c_ref[...], s_ref[...]
    k = (turn(k_ref[...], c, s) * (1.0 / math.sqrt(KEY_DIM))).astype(BF16)
    ko_ref[...] = k
    kin = (k.astype(F32) * powers(lg, rows - 1.0, rows, -1.0)).astype(BF16)
    end_ref[0] = dot(kin, v_ref[...], 0, 0)
    qo_ref[...] = turn(q_ref[...], c, s).astype(BF16)


def smem():
    return pl.BlockSpec(memory_space=pltpu.SMEM)


def keys(lg, q_raw, k_raw, v, c, s):
    rows = v.shape[0]
    heads = v.shape[1] // VAL_DIM
    narrow = pl.BlockSpec((rows, KEY_DIM), lambda h: (0, h))
    wide = pl.BlockSpec((rows, VAL_DIM), lambda h: (0, h))
    table = pl.BlockSpec((rows, KEY_DIM // 2), lambda h: (0, 0))
    state = pl.BlockSpec((1, KEY_DIM, VAL_DIM), lambda h: (h, 0, 0))
    return pl.pallas_call(
        keys_kernel,
        grid=(heads,),
        in_specs=[smem(), narrow, narrow, wide, table, table],
        out_specs=[narrow, narrow, state],
        out_shape=[
            jax.ShapeDtypeStruct(q_raw.shape, BF16),
            jax.ShapeDtypeStruct(k_raw.shape, BF16),
            jax.ShapeDtypeStruct((heads, KEY_DIM, VAL_DIM), F32),
        ],
        compiler_params=params(),
        cost_estimate=cost(heads * rows * KEY_DIM * VAL_DIM * 2, heads * rows * KEY_DIM * 24),
        name="retention_keys",
    )(lg, q_raw, k_raw, v, c, s)


def retain_kernel(lg_ref, q_ref, k_ref, v_ref, g_ref, st_ref, ret_ref, mix_ref):
    lg = lg_ref[pl.program_id(0)]
    rows = q_ref.shape[0]
    within = decay_within(lg, BLOCK)
    outward = powers(lg, 1.0, BLOCK, 1.0)
    inward = powers(lg, BLOCK - 1.0, BLOCK, -1.0)
    state = st_ref[0]
    for b in range(rows // BLOCK):
        at = slice(b * BLOCK, (b + 1) * BLOCK)
        q, k, v = q_ref[at, :], k_ref[at, :], v_ref[at, :]
        w = (dot(q, k, 1, 1) * within).astype(BF16)
        ret = dot(w, v, 1, 0) + outward * dot(q, state.astype(BF16), 1, 0)
        ret_ref[at, :] = ret
        c = ret - jnp.mean(ret, axis=1, keepdims=True)
        n = c * lax.rsqrt(jnp.mean(c * c, axis=1, keepdims=True) + GROUP_EPS)
        g = g_ref[at, :]
        mix_ref[at, :] = (g * jax.nn.sigmoid(g) * n).astype(BF16)
        if (b + 1) * BLOCK < rows:
            kin = (k.astype(F32) * inward).astype(BF16)
            state = jnp.exp(BLOCK * lg) * state + dot(kin, v, 0, 0)


def retain(lg, q, k, v, gate, state):
    rows = v.shape[0]
    heads = v.shape[1] // VAL_DIM
    narrow = pl.BlockSpec((rows, KEY_DIM), lambda h: (0, h))
    wide = pl.BlockSpec((rows, VAL_DIM), lambda h: (0, h))
    st = pl.BlockSpec((1, KEY_DIM, VAL_DIM), lambda h: (h, 0, 0))
    return pl.pallas_call(
        retain_kernel,
        grid=(heads,),
        in_specs=[smem(), narrow, narrow, wide, wide, st],
        out_specs=[wide, wide],
        out_shape=[jax.ShapeDtypeStruct(v.shape, F32), jax.ShapeDtypeStruct(v.shape, BF16)],
        compiler_params=params(),
        cost_estimate=cost(heads * rows * 1024 * 1024 * 2, heads * rows * VAL_DIM * 16),
        name="retention_forward",
    )(lg, q, k, v, gate, state)


def gate_back_kernel(lg_ref, q_ref, g_ref, ret_ref, gm_ref, gg_ref, gr_ref, first_ref):
    lg = lg_ref[pl.program_id(0)]
    i = pl.program_id(1)
    rows = q_ref.shape[0]
    ret = ret_ref[...]
    c = ret - jnp.mean(ret, axis=1, keepdims=True)
    rs = lax.rsqrt(jnp.mean(c * c, axis=1, keepdims=True) + GROUP_EPS)
    n = c * rs
    g = g_ref[...]
    sig = jax.nn.sigmoid(g)
    gm = gm_ref[...]
    gg_ref[...] = (gm * n * sig * (1.0 + g * (1.0 - sig))).astype(BF16)
    dn = gm * (g * sig)
    gr = rs * (dn - jnp.mean(dn, axis=1, keepdims=True) - n * jnp.mean(dn * n, axis=1, keepdims=True))
    gr = gr.astype(BF16)
    gr_ref[...] = gr
    scale = powers(lg, i.astype(F32) * rows + 1.0, rows, 1.0)
    part = dot(q_ref[...], (gr.astype(F32) * scale).astype(BF16), 0, 0)

    @pl.when(i == 0)
    def _():
        first_ref[0] = part

    @pl.when(i > 0)
    def _():
        first_ref[0] += part


def gate_back(lg, q, gate, ret, grad_mixed):
    rows = ret.shape[0]
    heads = ret.shape[1] // VAL_DIM
    tile = 256
    narrow = pl.BlockSpec((tile, KEY_DIM), lambda h, i: (i, h))
    wide = pl.BlockSpec((tile, VAL_DIM), lambda h, i: (i, h))
    st = pl.BlockSpec((1, KEY_DIM, VAL_DIM), lambda h, i: (h, 0, 0))
    return pl.pallas_call(
        gate_back_kernel,
        grid=(heads, rows // tile),
        in_specs=[smem(), narrow, wide, wide, wide],
        out_specs=[wide, wide, st],
        out_shape=[
            jax.ShapeDtypeStruct(ret.shape, BF16),
            jax.ShapeDtypeStruct(ret.shape, BF16),
            jax.ShapeDtypeStruct((heads, KEY_DIM, VAL_DIM), F32),
        ],
        compiler_params=params(),
        cost_estimate=cost(heads * rows * KEY_DIM * VAL_DIM * 2, heads * rows * VAL_DIM * 18),
        name="gate_back",
    )(lg, q, gate, ret, grad_mixed)


def retain_back_kernel(
    lg_ref, q_ref, k_ref, v_ref, gr_ref, st_ref, end_ref, c_ref, s_ref, dq_ref, dk_ref, dv_ref
):
    lg = lg_ref[pl.program_id(0)]
    rows = q_ref.shape[0]
    count = rows // BLOCK
    within = decay_within(lg, BLOCK)
    outward = powers(lg, 1.0, BLOCK, 1.0)
    inward = powers(lg, BLOCK - 1.0, BLOCK, -1.0)
    whole = jnp.exp(BLOCK * lg)
    spans = [slice(b * BLOCK, (b + 1) * BLOCK) for b in range(count)]
    states = [st_ref[0]]
    for at in spans[:-1]:
        kin = (k_ref[at, :].astype(F32) * inward).astype(BF16)
        states.append(whole * states[-1] + dot(kin, v_ref[at, :], 0, 0))
    after = end_ref[0]
    for b in range(count - 1, -1, -1):
        at = spans[b]
        q, k, v, gr = q_ref[at, :], k_ref[at, :], v_ref[at, :], gr_ref[at, :]
        c, s = c_ref[at, :], s_ref[at, :]
        late = after.astype(BF16)
        w = (dot(q, k, 1, 1) * within).astype(BF16)
        gs = (dot(gr, v, 1, 1) * within).astype(BF16)
        kin = (k.astype(F32) * inward).astype(BF16)
        dv_ref[at, :] = (dot(w, gr, 0, 0) + dot(kin, late, 1, 0)).astype(BF16)
        dq = dot(gs, k, 1, 0) + outward * dot(gr, states[b].astype(BF16), 1, 1)
        dq_ref[at, :] = turn_back(dq, c, s).astype(BF16)
        dk = dot(gs, q, 0, 0) + inward * dot(v, late, 1, 1)
        dk_ref[at, :] = (turn_back(dk, c, s) * (1.0 / math.sqrt(KEY_DIM))).astype(BF16)
        if b:
            scaled = (gr.astype(F32) * outward).astype(BF16)
            after = whole * after + dot(q, scaled, 0, 0)


def retain_back(lg, q, k, v, gr, state, end, c, s):
    rows = v.shape[0]
    heads = v.shape[1] // VAL_DIM
    narrow = pl.BlockSpec((rows, KEY_DIM), lambda h: (0, h))
    wide = pl.BlockSpec((rows, VAL_DIM), lambda h: (0, h))
    st = pl.BlockSpec((1, KEY_DIM, VAL_DIM), lambda h: (h, 0, 0))
    table = pl.BlockSpec((rows, KEY_DIM // 2), lambda h: (0, 0))
    return pl.pallas_call(
        retain_back_kernel,
        grid=(heads,),
        in_specs=[smem(), narrow, narrow, wide, wide, st, st, table, table],
        out_specs=[narrow, narrow, wide],
        out_shape=[
            jax.ShapeDtypeStruct(q.shape, BF16),
            jax.ShapeDtypeStruct(k.shape, BF16),
            jax.ShapeDtypeStruct(v.shape, BF16),
        ],
        compiler_params=params(),
        cost_estimate=cost(heads * rows * 1024 * 1024 * 5, heads * rows * VAL_DIM * 12),
        name="retention_back",
    )(lg, q, k, v, gr, state, end, c, s)


def entering(own, lg, rows, per_seq, me, backward):
    total = own
    state = jnp.zeros_like(own)
    bit = 1
    while bit < per_seq:
        got = swap(total.astype(BF16), bit).astype(F32)
        place = lax.bitwise_and(me, bit - 1)
        upper = lax.bitwise_and(me, bit) != 0
        if backward:
            gap = (bit - 1) - place
            takes = jnp.logical_not(upper)
        else:
            gap = place
            takes = upper
        far = jnp.exp(rows * bit * lg)[:, None, None]
        near = jnp.exp(rows * gap.astype(F32) * lg)[:, None, None]
        state = state + jnp.where(takes, near, 0.0) * got
        if bit * 2 < per_seq:
            total = jnp.where(takes, total + far * got, far * total + got)
        bit *= 2
    return state


def place_kernel(ids, a_ref, o_ref):
    o_ref[...] = a_ref[0].astype(F32)


def place(ids, pieces):
    n = len(pieces)
    rows, d = pieces[0].shape
    return pl.pallas_call(
        place_kernel,
        grid_spec=pltpu.PrefetchScalarGridSpec(
            num_scalar_prefetch=1,
            grid=(n,),
            in_specs=[
                pl.BlockSpec((1, rows, d), lambda i, ids: (lax.bitwise_xor(ids[0], i), 0, 0))
            ],
            out_specs=pl.BlockSpec((rows, d), lambda i, ids: (i, 0)),
        ),
        out_shape=jax.ShapeDtypeStruct((n * rows, d), F32),
        compiler_params=params(),
        cost_estimate=cost(0, n * rows * d * 6),
        name="place_rows",
    )(ids, jnp.stack([pieces[j] for j in range(n)]))


def grad_rows(left, right, n_seq, flip):
    half = left.shape[1] // 2
    size = left.shape[1] // n_seq
    got = swap(dot(left[:, half:], right, 0, 0).astype(BF16), 1)
    kept = dot(left[:, :half], right, 0, 0) + got.astype(F32)
    pieces = {2 * p: kept[p * size : (p + 1) * size] for p in range(n_seq // 2)}
    return xor_finish(pieces, flip)


def grad_columns(left, right, n_seq, flip):
    half = right.shape[1] // 2
    size = right.shape[1] // n_seq
    got = swap(dot(left, right[:, half:], 0, 0).astype(BF16), 1)
    kept = dot(left, right[:, :half], 0, 0) + got.astype(F32)
    pieces = {2 * p: kept[:, p * size : (p + 1) * size] for p in range(n_seq // 2)}
    return xor_finish(pieces, flip)


def token_sum(left, right, n_seq, flip):
    half = left.shape[0] // 2
    size = left.shape[0] // n_seq
    got = swap(dot(left[half:], right, 1, 0).astype(BF16), 1)
    kept = dot(left[:half], right, 1, 0) + got.astype(F32)
    pieces = {2 * p: kept[p * size : (p + 1) * size] for p in range(n_seq // 2)}
    return xor_finish(pieces, flip)


def local(
    layer_input,
    gain_one,
    query_weight,
    key_weight,
    value_weight,
    gate_weight,
    out_weight,
    gain_two,
    up_weight,
    down_weight,
    cotangent,
):
    rows, d_part = layer_input.shape
    n_seq = lax.axis_size("seq")
    n_tp = lax.axis_size("tp")
    d = d_part * n_tp
    me = lax.axis_index("seq").astype(jnp.int32)
    t = lax.axis_index("tp").astype(jnp.int32)
    ids = jnp.stack([me, t])
    heads = query_weight.shape[1] // KEY_DIM
    own_rows = rows // n_tp
    seq_length = min(MAXLEN, rows * n_seq)
    per_seq = max(seq_length // rows, 1)
    order = order_of(n_seq)

    x_full = lax.all_gather(layer_input, "tp", axis=1, tiled=True)

    w_pieces = [
        xor_gather(w, i % 2 == 1)
        for i, w in enumerate((query_weight, key_weight, value_weight, gate_weight))
    ]
    query_full, key_full, value_full, gate_full = [
        jnp.concatenate([p[j] for j in order], axis=0) for p in w_pieces
    ]
    half_out = out_weight.shape[0] // 2
    out_pieces = [xor_gather(out_weight[:half_out], False), xor_gather(out_weight[half_out:], True)]
    out_full = jnp.concatenate(
        [jnp.concatenate([p[j] for j in order], axis=1) for p in out_pieces], axis=0
    )

    gains = {0: jnp.stack([gain_one, gain_two])}
    bit = 1
    while bit < n_tp:
        for j in list(gains):
            gains[j ^ bit] = swap(gains[j], bit, "tp")
        bit *= 2
    gains = jnp.stack([gains[j] for j in range(n_tp)])[lax.bitwise_xor(t, jnp.arange(n_tp))]
    gains = gains.transpose(1, 0, 2).reshape(2, d)
    gain_one_full, gain_two_full = gains[0:1], gains[1:2]

    cot_rows = jnp.zeros((own_rows, d), BF16)
    for j in range(n_tp):
        to = lax.bitwise_xor(t, j)
        block = lax.dynamic_slice_in_dim(cotangent, to * own_rows, own_rows, 0)
        if j:
            block = swap(block, j, "tp")
        cot_rows = lax.dynamic_update_slice(cot_rows, block, (jnp.int32(0), to * d_part))
    half_rows = own_rows // 2
    cot_parts = []
    for i in range(2):
        p = xor_gather(cot_rows[i * half_rows : (i + 1) * half_rows], i == 1)
        cot_parts.append(jnp.concatenate([p[j] for j in order], axis=0))

    units = up_weight.shape[1] // n_seq
    up_own = lax.dynamic_slice_in_dim(up_weight, me * units, units, 1).T
    down_own = lax.dynamic_slice_in_dim(down_weight, me * units, units, 0)
    up_t = lax.all_gather(up_own, "tp", axis=0, tiled=True)
    down = lax.all_gather(down_own, "tp", axis=0, tiled=True)

    head_ids = t * heads + jnp.arange(heads)
    lg = jnp.log(1.0 - jnp.exp2(-5.0 - head_ids.astype(F32)))
    first = (me * rows) % seq_length
    half_key = KEY_DIM // 2
    freq = jnp.exp(-math.log(10000.0) * jnp.arange(half_key, dtype=F32) / half_key)
    angles = (first + jnp.arange(rows)).astype(F32)[:, None] * freq[None, :]
    cos, sin = jnp.cos(angles), jnp.sin(angles)

    shared = norm_one(ids, x_full, gain_one_full, n_seq)
    q_raw = dot(shared, query_full, 1, 0)
    k_raw = dot(shared, key_full, 1, 0)
    value = dot(shared, value_full, 1, 0).astype(BF16)
    query, key, own_end = keys(lg, q_raw, k_raw, value, cos, sin)
    state_in = entering(own_end, lg, rows, per_seq, me, False)
    gate = dot(shared, gate_full, 1, 0)
    retained, mixed = retain(lg, query, key, value, gate, state_in)
    branch = dot(mixed, out_full, 1, 0).astype(BF16)
    branch = lax.psum_scatter(branch, "tp", scatter_dimension=0, tiled=True)
    hidden, norm_a, norm_b = norm_two(ids, branch, x_full, gain_two_full, n_seq)

    parts = []
    for i, a in enumerate((norm_a, norm_b)):
        p = xor_gather(a, i == 1)
        parts.append(jnp.concatenate([p[j] for j in order], axis=0))
    grad_acts = [dot(c, down, 1, 1) for c in cot_parts]
    acts, grad_ups, grads_two, ffn = [], [], [], []
    for i in range(2):
        up_pre = dot(parts[i], up_t, 1, 1)
        act, pull = jax.vjp(jax.nn.gelu, up_pre)
        acts.append(act.astype(BF16))
        grad_ups.append(pull(grad_acts[i])[0].astype(BF16))
        grads_two.append(token_sum(grad_ups[i], up_t, n_seq, i == 1))
    for i in range(2):
        ffn.append(token_sum(acts[i], down, n_seq, i == 1))

    out_rows = (hidden + jnp.concatenate(ffn, axis=0)).astype(BF16)
    layer_output = jnp.zeros((rows, d_part), BF16)
    for j in range(n_tp):
        to = lax.bitwise_xor(t, j)
        block = lax.dynamic_slice_in_dim(out_rows, to * d_part, d_part, 1)
        if j:
            block = swap(block, j, "tp")
        layer_output = lax.dynamic_update_slice(layer_output, block, (to * own_rows, jnp.int32(0)))

    up_grad = sum(dot(g, n, 0, 0) for g, n in zip(grad_ups, parts)).astype(BF16)
    down_grad = sum(dot(a, c, 0, 0) for a, c in zip(acts, cot_parts)).astype(BF16)
    up_grad = lax.psum_scatter(up_grad, "tp", scatter_dimension=0, tiled=True)
    down_grad = lax.psum_scatter(down_grad, "tp", scatter_dimension=0, tiled=True)
    up_grad = place(ids, xor_gather(up_grad, False)).T
    down_grad = place(ids, xor_gather(down_grad, True))

    grad_hidden, grad_branch, gain_two_part = norm_two_back(
        ids, grads_two[0], grads_two[1], hidden, cot_rows, gain_two_full, n_seq
    )

    grad_branch = lax.all_gather(grad_branch, "tp", axis=0, tiled=True)
    grad_mixed = dot(grad_branch, out_full, 1, 1)
    grad_gate, grad_ret, own_first = gate_back(lg, query, gate, retained, grad_mixed)
    grad_end = entering(own_first, lg, rows, per_seq, me, True)
    out_grad = jnp.concatenate(
        [
            grad_columns(mixed[:, i * half_out : (i + 1) * half_out], grad_branch, n_seq, i == 1)
            for i in range(2)
        ],
        axis=0,
    )
    gate_grad = grad_rows(shared, grad_gate, n_seq, True)
    dq, dk, dv = retain_back(lg, query, key, value, grad_ret, state_in, grad_end, cos, sin)
    grad_shared = (
        dot(grad_gate, gate_full, 1, 1)
        + dot(dv, value_full, 1, 1)
        + dot(dq, query_full, 1, 1)
        + dot(dk, key_full, 1, 1)
    )
    grad_x, gain_one_part = norm_one_back(ids, grad_shared, x_full, gain_one_full, grad_hidden, n_seq)
    input_grad = lax.psum_scatter(grad_x, "tp", scatter_dimension=1, tiled=True)
    value_grad = grad_rows(shared, dv, n_seq, False)
    query_grad = grad_rows(shared, dq, n_seq, False)
    key_grad = grad_rows(shared, dk, n_seq, True)

    sums = jnp.concatenate([gain_one_part, gain_two_part], axis=0)
    for axis, n in (("tp", n_tp), ("seq", n_seq)):
        bit = 1
        while bit < n:
            sums = sums + swap(sums, bit, axis)
            bit *= 2
    sums = lax.dynamic_slice_in_dim(sums, t * d_part, d_part, 1)

    return (
        layer_output,
        input_grad,
        sums[0],
        query_grad,
        key_grad,
        value_grad,
        gate_grad,
        out_grad,
        sums[1],
        up_grad,
        down_grad,
    )


def solution(mesh):
    placed = (
        P("seq", "tp"),
        P("tp"),
        P("seq", "tp"),
        P("seq", "tp"),
        P("seq", "tp"),
        P("seq", "tp"),
        P("tp", "seq"),
        P("tp"),
        P(None, "tp"),
        P("tp", None),
        P("seq", "tp"),
    )
    return jax.shard_map(
        local,
        mesh=mesh,
        in_specs=placed,
        out_specs=(
            P("seq", "tp"),
            P("seq", "tp"),
            P("tp"),
            P("seq", "tp"),
            P("seq", "tp"),
            P("seq", "tp"),
            P("seq", "tp"),
            P("tp", "seq"),
            P("tp"),
            P(None, "tp"),
            P("tp", None),
        ),
        check_vma=False,
    )
```

```python
import functools
import math

import jax
import jax.numpy as jnp
from jax import lax
from jax.experimental import pallas as pl
from jax.experimental.pallas import tpu as pltpu
from jax.sharding import PartitionSpec as P


KEY_DIM = 256
VAL_DIM = 512
BLOCK = 512
MAXLEN = 8192
NORM_EPS = 1e-05
GROUP_EPS = 1.0
F32 = jnp.float32
BF16 = jnp.bfloat16
VMEM_LIMIT = 56 * 1024 * 1024


def dot(a, b, ca, cb):
    return lax.dot_general(a, b, (((ca,), (cb,)), ((), ())), preferred_element_type=F32)


def params(**kw):
    return pltpu.CompilerParams(vmem_limit_bytes=VMEM_LIMIT, **kw)


def cost(flops, nbytes):
    return pl.CostEstimate(flops=int(flops), bytes_accessed=int(nbytes), transcendentals=0)


def swap(a, bit, axis="seq"):
    n = lax.axis_size(axis)
    return lax.ppermute(a, axis, [(i, i ^ bit) for i in range(n)])


def outer_bits(flip):
    bits = [1 << k for k in range(1, (lax.axis_size("seq") - 1).bit_length())]
    return bits[::-1] if flip else bits


def xor_gather(a, flip):
    pieces = {0: a}
    for bit in outer_bits(flip) + [1]:
        for j in list(pieces):
            pieces[j ^ bit] = swap(pieces[j], bit)
    return pieces


def order_of(n):
    return [j for j in range(n) if j % 2 == 0] + [j for j in range(n) if j % 2 == 1]


def after(x, *deps):
    return lax.optimization_barrier((x,) + deps)[0]


def row_norm(x):
    mean = jnp.mean(x, axis=1, keepdims=True)
    c = x - mean
    r = lax.rsqrt(jnp.mean(c * c, axis=1, keepdims=True) + NORM_EPS)
    return c * r, r


def block_at(ids, j, size):
    return pl.ds(pl.multiple_of(lax.bitwise_xor(ids[0], jnp.int32(j)) * size, size), size)


def turn(v, c, s):
    h = v.shape[1] // 2
    a, b = v[:, :h], v[:, h:]
    return jnp.concatenate([a * c - b * s, a * s + b * c], axis=1)


def turn_back(v, c, s):
    h = v.shape[1] // 2
    a, b = v[:, :h], v[:, h:]
    return jnp.concatenate([a * c + b * s, b * c - a * s], axis=1)


def powers(lg, start, count, step):
    at = lax.broadcasted_iota(jnp.int32, (count, 1), 0).astype(F32)
    return jnp.exp((start + step * at) * lg)


def decay_within(lg, size):
    lag = lax.broadcasted_iota(jnp.int32, (size, size), 0) - lax.broadcasted_iota(
        jnp.int32, (size, size), 1
    )
    return jnp.where(lag >= 0, jnp.exp(jnp.maximum(lag, 0).astype(F32) * lg), 0.0)


def head(h, size):
    return slice(h * size, (h + 1) * size)


def anywhere(n):
    return [pl.BlockSpec(memory_space=pl.ANY) for _ in range(n)]


def smem():
    return pl.BlockSpec(memory_space=pltpu.SMEM)


def columns_in(refs, cols, w, to, rows_of, sem, base):
    copies = []
    for j, ref in enumerate(refs):
        copies.append(
            pltpu.make_async_copy(
                ref.at[:, cols], w.at[rows_of(j), to : to + cols.stop - cols.start], sem.at[base + j]
            )
        )
    return copies


def relative_rows(order, size):
    return lambda j: slice(order.index(j) * size, (order.index(j) + 1) * size)


def key_value_kernel(order, heads, ids, lg_ref, x_ref, gain_ref, c_ref, s_ref, *refs):
    n = len(order)
    a, b = refs[:n], refs[n : 2 * n]
    sh_ref, key_ref, val_ref, end_ref, w, tmp, sem = refs[2 * n :]
    kq, vv = heads * KEY_DIM, heads * VAL_DIM
    i = pl.program_id(0)
    tile, d = x_ref.shape
    size = d // n
    total = tile * pl.num_programs(0)
    rows_of = relative_rows(order, size)
    copies = columns_in(b, slice(0, kq), w, 0, rows_of, sem, 0)
    copies += columns_in(a, slice(kq, kq + vv), w, kq, rows_of, sem, n)

    @pl.when(i == 0)
    def _():
        for copy in copies:
            copy.start()

    nrm, _ = row_norm(x_ref[...].astype(F32))
    tmp[...] = (nrm * gain_ref[...]).astype(BF16)
    for p, j in enumerate(order):
        sh_ref[:, p * size : (p + 1) * size] = tmp[:, block_at(ids, j, size)]

    @pl.when(i == 0)
    def _():
        for copy in copies:
            copy.wait()

    r = dot(sh_ref[...], w[...], 1, 0)
    c, s = c_ref[...], s_ref[...]
    val_ref[...] = r[:, kq:].astype(BF16)
    for h in range(heads):
        lg = lg_ref[h]
        k = (turn(r[:, head(h, KEY_DIM)], c, s) * (1.0 / math.sqrt(KEY_DIM))).astype(BF16)
        key_ref[:, head(h, KEY_DIM)] = k
        start = (total - 1 - i * tile).astype(F32)
        kin = (k.astype(F32) * powers(lg, start, tile, -1.0)).astype(BF16)
        part = dot(kin, val_ref[:, head(h, VAL_DIM)], 0, 0)

        @pl.when(i == 0)
        def _():
            end_ref[h] = part

        @pl.when(i > 0)
        def _():
            end_ref[h] += part


def step_spec(tile, width):
    return pl.BlockSpec((tile, width), lambda i, ids: (i, 0))


def fixed_spec(*shape):
    return pl.BlockSpec(shape, lambda i, ids: (0,) * len(shape))


def key_value(ids, lg, x, gain, c, s, a, b):
    rows, d = x.shape
    n = len(a)
    heads = lg.shape[0]
    kq, vv = heads * KEY_DIM, heads * VAL_DIM
    tile = 256
    return pl.pallas_call(
        functools.partial(key_value_kernel, order_of(n), heads),
        grid_spec=pltpu.PrefetchScalarGridSpec(
            num_scalar_prefetch=1,
            grid=(rows // tile,),
            in_specs=[smem(), step_spec(tile, d), fixed_spec(1, d)]
            + [step_spec(tile, KEY_DIM // 2)] * 2
            + anywhere(2 * n),
            out_specs=[
                step_spec(tile, d),
                step_spec(tile, kq),
                step_spec(tile, vv),
                fixed_spec(heads, KEY_DIM, VAL_DIM),
            ],
            scratch_shapes=[
                pltpu.VMEM((d, kq + vv), BF16),
                pltpu.VMEM((tile, d), BF16),
                pltpu.SemaphoreType.DMA((2 * n,)),
            ],
        ),
        out_shape=[
            jax.ShapeDtypeStruct((rows, d), BF16),
            jax.ShapeDtypeStruct((rows, kq), BF16),
            jax.ShapeDtypeStruct((rows, vv), BF16),
            jax.ShapeDtypeStruct((heads, KEY_DIM, VAL_DIM), F32),
        ],
        compiler_params=params(),
        cost_estimate=cost(rows * d * (kq + vv) * 2, (rows * d * 3 + d * (kq + vv)) * 2),
        name="kv",
    )(ids, lg, x, gain, c, s, *a, *b)


def query_gate_kernel(order, heads, ids, sh_ref, c_ref, s_ref, *refs):
    n = len(order)
    a, b = refs[:n], refs[n : 2 * n]
    q_ref, g_ref, w, sem = refs[2 * n :]
    kq, vv = heads * KEY_DIM, heads * VAL_DIM
    rows_of = relative_rows(order, sh_ref.shape[1] // n)
    copies = columns_in(a, slice(0, kq), w, 0, rows_of, sem, 0)
    copies += columns_in(b, slice(kq, kq + vv), w, kq, rows_of, sem, n)

    @pl.when(pl.program_id(0) == 0)
    def _():
        for copy in copies:
            copy.start()
        for copy in copies:
            copy.wait()

    r = dot(sh_ref[...], w[...], 1, 0)
    g_ref[...] = r[:, kq:]
    c, s = c_ref[...], s_ref[...]
    for h in range(heads):
        q_ref[:, head(h, KEY_DIM)] = turn(r[:, head(h, KEY_DIM)], c, s).astype(BF16)


def query_gate(ids, shared, c, s, a, b, heads):
    rows, d = shared.shape
    n = len(a)
    kq, vv = heads * KEY_DIM, heads * VAL_DIM
    tile = 256
    return pl.pallas_call(
        functools.partial(query_gate_kernel, order_of(n), heads),
        grid_spec=pltpu.PrefetchScalarGridSpec(
            num_scalar_prefetch=1,
            grid=(rows // tile,),
            in_specs=[step_spec(tile, d)] + [step_spec(tile, KEY_DIM // 2)] * 2 + anywhere(2 * n),
            out_specs=[step_spec(tile, kq), step_spec(tile, vv)],
            scratch_shapes=[pltpu.VMEM((d, kq + vv), BF16), pltpu.SemaphoreType.DMA((2 * n,))],
        ),
        out_shape=[
            jax.ShapeDtypeStruct((rows, kq), BF16),
            jax.ShapeDtypeStruct((rows, vv), F32),
        ],
        compiler_params=params(),
        cost_estimate=cost(rows * d * (kq + vv) * 2, (rows * d * 2 + d * (kq + vv)) * 2),
        name="qu",
    )(ids, shared, c, s, *a, *b)


def retain_kernel(heads, n, blocks, ids, lg_ref, q_ref, k_ref, v_ref, g_ref, st_ref, *refs):
    a, b = refs[:n], refs[n : 2 * n]
    outs = refs[2 * n : 2 * n + 3 * blocks]
    state, acc, w, sem = refs[2 * n + 3 * blocks :]
    kq, vv = heads * KEY_DIM, heads * VAL_DIM
    size = w.shape[0] // n
    cols = slice(kq + vv, kq + vv + vv // 2)
    rows_of = lambda j: block_at(ids, j, size)
    copies = columns_in(a, cols, w, 0, rows_of, sem, 0)
    copies += columns_in(b, cols, w, vv // 2, rows_of, sem, n)
    blk, h = pl.program_id(0), pl.program_id(1)
    first = jnp.logical_and(blk == 0, h == 0)

    @pl.when(first)
    def _():
        for copy in copies:
            copy.start()

    @pl.when(blk == 0)
    def _():
        state[h] = st_ref[0]

    lg = lg_ref[h]
    outward = powers(lg, 1.0, BLOCK, 1.0)
    inward = powers(lg, BLOCK - 1.0, BLOCK, -1.0)
    q, k, v = q_ref[...], k_ref[...], v_ref[...]
    w_in = (dot(q, k, 1, 1) * decay_within(lg, BLOCK)).astype(BF16)
    ret = dot(w_in, v, 1, 0) + outward * dot(q, state[h].astype(BF16), 1, 0)
    c = ret - jnp.mean(ret, axis=1, keepdims=True)
    nrm = c * lax.rsqrt(jnp.mean(c * c, axis=1, keepdims=True) + GROUP_EPS)
    g = g_ref[...]
    mix = (g * jax.nn.sigmoid(g) * nrm).astype(BF16)

    @pl.when(blk + 1 < pl.num_programs(0))
    def _():
        kin = (k.astype(F32) * inward).astype(BF16)
        state[h] = jnp.exp(BLOCK * lg) * state[h] + dot(kin, v, 0, 0)

    @pl.when(first)
    def _():
        for copy in copies:
            copy.wait()

    part = dot(mix, w[:, pl.ds(pl.multiple_of(h * VAL_DIM, VAL_DIM), VAL_DIM)], 1, 1)

    @pl.when(h == 0)
    def _():
        acc[...] = part

    @pl.when(h > 0)
    def _():
        acc[...] += part

    at = pl.ds(pl.multiple_of(h * VAL_DIM, VAL_DIM), VAL_DIM)
    for i in range(blocks):
        ret_ref, mix_ref, br_ref = outs[i], outs[blocks + i], outs[2 * blocks + i]

        @pl.when(blk == i)
        def _():
            ret_ref[:, at] = ret
            mix_ref[:, at] = mix

        @pl.when(jnp.logical_and(blk == i, h == heads - 1))
        def _():
            br_ref[...] = acc[...].astype(BF16)


def retain(ids, lg, q, k, v, gate, state, a, b, d):
    rows = v.shape[0]
    n = len(a)
    heads = lg.shape[0]
    vv = heads * VAL_DIM
    blocks = rows // BLOCK
    narrow = pl.BlockSpec((BLOCK, KEY_DIM), lambda i, h, ids: (i, h))
    wide = pl.BlockSpec((BLOCK, VAL_DIM), lambda i, h, ids: (i, h))
    st = pl.BlockSpec((1, KEY_DIM, VAL_DIM), lambda i, h, ids: (h, 0, 0))
    fixed = lambda width: pl.BlockSpec((BLOCK, width), lambda i, h, ids: (0, 0))
    out = pl.pallas_call(
        functools.partial(retain_kernel, heads, n, blocks),
        grid_spec=pltpu.PrefetchScalarGridSpec(
            num_scalar_prefetch=1,
            grid=(blocks, heads),
            in_specs=[smem(), narrow, narrow, wide, wide, st] + anywhere(2 * n),
            out_specs=[fixed(vv)] * (2 * blocks) + [fixed(d)] * blocks,
            scratch_shapes=[
                pltpu.VMEM((heads, KEY_DIM, VAL_DIM), F32),
                pltpu.VMEM((BLOCK, d), F32),
                pltpu.VMEM((d, vv), BF16),
                pltpu.SemaphoreType.DMA((2 * n,)),
            ],
        ),
        out_shape=[jax.ShapeDtypeStruct((BLOCK, vv), F32)] * blocks
        + [jax.ShapeDtypeStruct((BLOCK, vv), BF16)] * blocks
        + [jax.ShapeDtypeStruct((BLOCK, d), BF16)] * blocks,
        compiler_params=params(),
        cost_estimate=cost(heads * rows * 3072 * 1024, rows * (heads * 8192 + d * 2)),
        name="rf",
    )(ids, lg, q, k, v, gate, state, *a, *b)
    return list(out[:blocks]), list(out[blocks : 2 * blocks]), list(out[2 * blocks :])


def gate_back_kernel(order, heads, base, ids, lg_ref, gb_ref, q_ref, g_ref, ret_ref, *refs):
    n = len(order)
    a, b = refs[:n], refs[n : 2 * n]
    gg_ref, gr_ref, first_ref, w, sem = refs[2 * n :]
    kq, vv = heads * KEY_DIM, heads * VAL_DIM
    i = pl.program_id(0)
    tile, d = gb_ref.shape
    cols = slice(kq + vv, kq + vv + vv // 2)
    rows_of = relative_rows(order, d // n)
    copies = columns_in(a, cols, w, 0, rows_of, sem, 0)
    copies += columns_in(b, cols, w, vv // 2, rows_of, sem, n)

    @pl.when(i == 0)
    def _():
        for copy in copies:
            copy.start()
        for copy in copies:
            copy.wait()

    for h in range(heads):
        at = head(h, VAL_DIM)
        lg = lg_ref[h]
        gm = dot(gb_ref[...], w[:, at], 1, 0)
        ret = ret_ref[:, at]
        c = ret - jnp.mean(ret, axis=1, keepdims=True)
        rs = lax.rsqrt(jnp.mean(c * c, axis=1, keepdims=True) + GROUP_EPS)
        nrm = c * rs
        g = g_ref[:, at]
        sig = jax.nn.sigmoid(g)
        gg_ref[:, at] = (gm * nrm * sig * (1.0 + g * (1.0 - sig))).astype(BF16)
        dn = gm * (g * sig)
        m1 = jnp.mean(dn, axis=1, keepdims=True)
        m2 = jnp.mean(dn * nrm, axis=1, keepdims=True)
        gr = (rs * (dn - m1 - nrm * m2)).astype(BF16)
        gr_ref[:, at] = gr
        scale = powers(lg, (i * tile + (base + 1)).astype(F32), tile, 1.0)
        part = dot(q_ref[:, head(h, KEY_DIM)], (gr.astype(F32) * scale).astype(BF16), 0, 0)

        @pl.when(i == 0)
        def _():
            first_ref[h] = part

        @pl.when(i > 0)
        def _():
            first_ref[h] += part


def gate_back(ids, lg, grad_branch, q, gate, ret, a, b, blk):
    rows, d = grad_branch.shape
    n = len(a)
    heads = lg.shape[0]
    kq, vv = heads * KEY_DIM, heads * VAL_DIM
    tile = 256
    return pl.pallas_call(
        functools.partial(gate_back_kernel, order_of(n), heads, blk * rows),
        grid_spec=pltpu.PrefetchScalarGridSpec(
            num_scalar_prefetch=1,
            grid=(rows // tile,),
            in_specs=[
                smem(),
                step_spec(tile, d),
                pl.BlockSpec((tile, kq), lambda i, ids: (i + blk * (rows // tile), 0)),
                pl.BlockSpec((tile, vv), lambda i, ids: (i + blk * (rows // tile), 0)),
                step_spec(tile, vv),
            ]
            + anywhere(2 * n),
            out_specs=[
                step_spec(tile, vv),
                step_spec(tile, vv),
                fixed_spec(heads, KEY_DIM, VAL_DIM),
            ],
            scratch_shapes=[pltpu.VMEM((d, vv), BF16), pltpu.SemaphoreType.DMA((2 * n,))],
        ),
        out_shape=[
            jax.ShapeDtypeStruct(ret.shape, BF16),
            jax.ShapeDtypeStruct(ret.shape, BF16),
            jax.ShapeDtypeStruct((heads, KEY_DIM, VAL_DIM), F32),
        ],
        compiler_params=params(),
        cost_estimate=cost(rows * d * vv * 2.5, rows * (d * 2 + vv * 12) + d * vv * 2),
        name="gk",
    )(ids, lg, grad_branch, q, gate, ret, *a, *b)


def retain_back_kernel(
    lg_ref, q_ref, k_ref, v_ref, st_ref, end_ref, c_ref, s_ref, *refs
):
    lg = lg_ref[pl.program_id(0)]
    rows = q_ref.shape[0]
    count = rows // BLOCK
    gr_refs, d_ref = refs[:count], refs[count]
    h = pl.program_id(0)
    heads = pl.num_programs(0)
    q_at = pl.ds(pl.multiple_of(h * KEY_DIM, KEY_DIM), KEY_DIM)
    k_at = pl.ds(pl.multiple_of((heads + h) * KEY_DIM, KEY_DIM), KEY_DIM)
    v_at = pl.ds(pl.multiple_of(heads * 2 * KEY_DIM + h * VAL_DIM, KEY_DIM), VAL_DIM)
    within = decay_within(lg, BLOCK)
    outward = powers(lg, 1.0, BLOCK, 1.0)
    inward = powers(lg, BLOCK - 1.0, BLOCK, -1.0)
    whole = jnp.exp(BLOCK * lg)
    spans = [slice(b * BLOCK, (b + 1) * BLOCK) for b in range(count)]
    states = [st_ref[0]]
    for at in spans[:-1]:
        kin = (k_ref[at, :].astype(F32) * inward).astype(BF16)
        states.append(whole * states[-1] + dot(kin, v_ref[at, :], 0, 0))
    late_state = end_ref[0]
    for b in range(count - 1, -1, -1):
        at = spans[b]
        q, k, v, gr = q_ref[at, :], k_ref[at, :], v_ref[at, :], gr_refs[b][...]
        c, s = c_ref[at, :], s_ref[at, :]
        late = late_state.astype(BF16)
        w = (dot(q, k, 1, 1) * within).astype(BF16)
        gs = (dot(gr, v, 1, 1) * within).astype(BF16)
        kin = (k.astype(F32) * inward).astype(BF16)
        d_ref[at, v_at] = (dot(w, gr, 0, 0) + dot(kin, late, 1, 0)).astype(BF16)
        dq = dot(gs, k, 1, 0) + outward * dot(gr, states[b].astype(BF16), 1, 1)
        d_ref[at, q_at] = turn_back(dq, c, s).astype(BF16)
        dk = dot(gs, q, 0, 0) + inward * dot(v, late, 1, 1)
        d_ref[at, k_at] = (turn_back(dk, c, s) * (1.0 / math.sqrt(KEY_DIM))).astype(BF16)
        if b:
            scaled = (gr.astype(F32) * outward).astype(BF16)
            late_state = whole * late_state + dot(q, scaled, 0, 0)


def retain_back(lg, q, k, v, gr, state, end, c, s):
    rows = v.shape[0]
    heads = v.shape[1] // VAL_DIM
    narrow = pl.BlockSpec((rows, KEY_DIM), lambda h: (0, h))
    wide = pl.BlockSpec((rows, VAL_DIM), lambda h: (0, h))
    st = pl.BlockSpec((1, KEY_DIM, VAL_DIM), lambda h: (h, 0, 0))
    table = pl.BlockSpec((rows, KEY_DIM // 2), lambda h: (0, 0))
    return pl.pallas_call(
        retain_back_kernel,
        grid=(heads,),
        in_specs=[smem(), narrow, narrow, wide, st, st, table, table]
        + [pl.BlockSpec((BLOCK, VAL_DIM), lambda h: (0, h))] * len(gr),
        out_specs=pl.BlockSpec((rows, heads * (2 * KEY_DIM + VAL_DIM)), lambda h: (0, 0)),
        out_shape=jax.ShapeDtypeStruct((rows, heads * (2 * KEY_DIM + VAL_DIM)), BF16),
        compiler_params=params(),
        cost_estimate=cost(heads * rows * 1024 * 1024 * 5, heads * rows * VAL_DIM * 12),
        name="rb",
    )(lg, q, k, v, state, end, c, s, *gr)


def input_back_kernel(heads, n, blocks, ids, d_ref, x_ref, gain_ref, *refs):
    dg_refs, gh_refs = refs[:blocks], refs[blocks : 2 * blocks]
    a, b = refs[2 * blocks : 2 * blocks + n], refs[2 * blocks + n : 2 * blocks + 2 * n]
    o_ref, gg_ref, w, dg, tmp, sem = refs[2 * blocks + 2 * n :]
    kq, vv = heads * KEY_DIM, heads * VAL_DIM
    i = pl.program_id(0)
    tile, d = x_ref.shape
    size = d // n
    rows_of = lambda j: block_at(ids, j, size)
    copies = columns_in(a, slice(0, kq), w, 0, rows_of, sem, 0)
    copies += columns_in(b, slice(0, kq), w, kq, rows_of, sem, n)
    copies += columns_in(a, slice(kq, kq + vv), w, 2 * kq, rows_of, sem, 2 * n)
    copies += columns_in(b, slice(kq, kq + vv), w, 2 * kq + vv, rows_of, sem, 3 * n)

    @pl.when(i == 0)
    def _():
        for copy in copies:
            copy.start()
        for copy in copies:
            copy.wait()

    for k in range(blocks):

        @pl.when(i // (BLOCK // tile) == k)
        def _():
            dg[...] = dg_refs[k][...]

    grads = jnp.concatenate([d_ref[...], dg[...]], axis=1)
    g = dot(grads, w[...], 1, 1)
    nrm, r = row_norm(x_ref[...].astype(F32))
    part = jnp.sum(g * nrm, axis=0, keepdims=True)

    @pl.when(i == 0)
    def _():
        gg_ref[...] = part

    @pl.when(i > 0)
    def _():
        gg_ref[...] += part

    e = g * gain_ref[...]
    m1 = jnp.mean(e, axis=1, keepdims=True)
    m2 = jnp.mean(e * nrm, axis=1, keepdims=True)
    back = r * (e - m1 - nrm * m2)
    o_ref[...] = back.astype(BF16)
    own = gh_refs[0].shape[0]
    for k in range(blocks):

        @pl.when(i == (k * BLOCK + ids[1] * own) // tile)
        def _():
            tmp[...] = back
            at = pl.ds(pl.multiple_of(lax.rem(ids[1] * own, tile), own), own)
            o_ref[at, :] = (tmp[at, :] + gh_refs[k][...]).astype(BF16)


def input_back(ids, dqkv, dg, x, gain, grad_hidden, a, b):
    rows, d = x.shape
    n = len(a)
    vv = dg[0].shape[1]
    heads = vv // VAL_DIM
    kq = heads * KEY_DIM
    blocks = len(dg)
    tile = 256
    steps = BLOCK // tile
    return pl.pallas_call(
        functools.partial(input_back_kernel, heads, n, blocks),
        grid_spec=pltpu.PrefetchScalarGridSpec(
            num_scalar_prefetch=1,
            grid=(rows // tile,),
            in_specs=[
                step_spec(tile, 2 * kq + vv),
                step_spec(tile, d),
                fixed_spec(1, d),
            ]
            + [
                pl.BlockSpec(
                    (tile, vv), lambda i, ids, k=k: (jnp.clip(i - k * steps, 0, steps - 1), 0)
                )
                for k in range(blocks)
            ]
            + [fixed_spec(*g.shape) for g in grad_hidden]
            + anywhere(2 * n),
            out_specs=[step_spec(tile, d), fixed_spec(1, d)],
            scratch_shapes=[
                pltpu.VMEM((d, 2 * (kq + vv)), BF16),
                pltpu.VMEM((tile, vv), BF16),
                pltpu.VMEM((tile, d), F32),
                pltpu.SemaphoreType.DMA((4 * n,)),
            ],
        ),
        out_shape=[jax.ShapeDtypeStruct((rows, d), BF16), jax.ShapeDtypeStruct((1, d), F32)],
        compiler_params=params(),
        cost_estimate=cost(rows * d * (kq + vv) * 4, (rows + d) * 2 * (kq + vv) * 2 + rows * d * 4),
        name="ib",
    )(ids, dqkv, x, gain, *dg, *grad_hidden, *a, *b)


def norm_two_kernel(ids, r_ref, x_ref, gain_ref, h_ref, n_ref):
    hidden = x_ref[...].astype(F32) + r_ref[...].astype(F32)
    h_ref[...] = hidden
    n, _ = row_norm(hidden)
    n_ref[...] = (n * gain_ref[...]).astype(BF16)


def norm_two(ids, r, x, gain, blk, n_tp):
    rows, d = r.shape
    return pl.pallas_call(
        norm_two_kernel,
        grid_spec=pltpu.PrefetchScalarGridSpec(
            num_scalar_prefetch=1,
            grid=(1,),
            in_specs=[
                fixed_spec(rows, d),
                pl.BlockSpec((rows, d), lambda i, ids: (ids[1] + blk * n_tp, 0)),
                fixed_spec(1, d),
            ],
            out_specs=[fixed_spec(rows, d), fixed_spec(rows, d)],
        ),
        out_shape=[jax.ShapeDtypeStruct((rows, d), F32), jax.ShapeDtypeStruct((rows, d), BF16)],
        compiler_params=params(),
        cost_estimate=cost(rows * d * 10, rows * d * 10),
        name="na",
    )(ids, r, x, gain)


def norm_two_back_kernel(order, ids, g_ref, h_ref, cot_ref, gain_ref, gh_ref, br_ref, gg_ref):
    size = h_ref.shape[1] // len(order)
    n, r = row_norm(h_ref[...])
    g = g_ref[...]
    gg_ref[...] = jnp.sum(g * n, axis=0, keepdims=True)
    e = g * gain_ref[...]
    back = r * (e - jnp.mean(e, axis=1, keepdims=True) - n * jnp.mean(e * n, axis=1, keepdims=True))
    gh_ref[...] = cot_ref[...].astype(F32) + back
    for p, j in enumerate(order):
        br_ref[:, p * size : (p + 1) * size] = gh_ref[:, block_at(ids, j, size)].astype(BF16)


def norm_two_back(ids, g, hidden, cot, gain, n_seq):
    rows, d = hidden.shape
    whole = fixed_spec(rows, d)
    return pl.pallas_call(
        functools.partial(norm_two_back_kernel, order_of(n_seq)),
        grid_spec=pltpu.PrefetchScalarGridSpec(
            num_scalar_prefetch=1,
            grid=(1,),
            in_specs=[whole, whole, whole, fixed_spec(1, d)],
            out_specs=[whole, whole, fixed_spec(1, d)],
        ),
        out_shape=[
            jax.ShapeDtypeStruct((rows, d), F32),
            jax.ShapeDtypeStruct((rows, d), BF16),
            jax.ShapeDtypeStruct((1, d), F32),
        ],
        compiler_params=params(),
        cost_estimate=cost(rows * d * 20, rows * d * 16),
        name="nb",
    )(ids, g, hidden, cot, gain)


def plane_gather(a):
    n = lax.axis_size("seq")
    even = [a] + [swap(a, j) for j in range(2, n, 2)]
    return even, [swap(p, 1) for p in even]


def chip_sum(even, odd):
    return even.astype(F32) + swap(odd, 1).astype(F32)


def plane_sum(total, last=None):
    n = lax.axis_size("seq")
    size = total.shape[0] // (n // 2)
    pieces = [total[i * size : (i + 1) * size] for i in range(n // 2)]
    own = pieces[0] if last is None else after(pieces[0], last)
    return own + sum(swap(p.astype(BF16), 2 * i).astype(F32) for i, p in enumerate(pieces) if i)


def plane_reduce(even, odd, last=None):
    return plane_sum(chip_sum(even, odd), last)


def rows_joined(refs):
    return jnp.concatenate([r[...] for r in refs], axis=0)


def grad_act_kernel(m, *refs):
    refs[m + 1][...] = dot(rows_joined(refs[:m]), refs[m][0], 1, 1)


def full(*shape):
    return pl.BlockSpec(shape, lambda i: (0,) * len(shape))


def ffn_part(ffn_w, k):
    return pl.BlockSpec((1,) + ffn_w.shape[1:], lambda i: (k, 0, 0))


def grad_act(pieces, ffn_w):
    rows = sum(p.shape[0] for p in pieces)
    _, units, d = ffn_w.shape
    return pl.pallas_call(
        functools.partial(grad_act_kernel, len(pieces)),
        grid=(1,),
        in_specs=[full(*p.shape) for p in pieces] + [ffn_part(ffn_w, 1)],
        out_specs=full(rows, units),
        out_shape=jax.ShapeDtypeStruct((rows, units), F32),
        compiler_params=params(),
        cost_estimate=cost(rows * d * units * 2, rows * d * 2 + units * d * 2),
        name="ga",
    )(*pieces, ffn_w)


def feed_kernel(m, *refs):
    ga_ref, up_ref, out_ref, act_ref, gu_ref = refs[m:]
    up = dot(rows_joined(refs[:m]), up_ref[0], 1, 1)
    c0 = math.sqrt(2.0 / math.pi)
    th = jnp.tanh(c0 * (up + 0.044715 * up * up * up))
    act_ref[...] = (0.5 * up * (1.0 + th)).astype(BF16)
    slope = 0.5 * (1.0 + th) + 0.5 * up * (1.0 - th * th) * c0 * (1.0 + 0.134145 * up * up)
    gu = (ga_ref[...] * slope).astype(BF16)
    gu_ref[...] = gu
    out_ref[...] = dot(gu, up_ref[0], 1, 0).astype(BF16)


def feed(pieces, grad, ffn_w):
    rows = sum(p.shape[0] for p in pieces)
    _, units, d = ffn_w.shape
    return pl.pallas_call(
        functools.partial(feed_kernel, len(pieces)),
        grid=(1,),
        in_specs=[full(*p.shape) for p in pieces] + [full(rows, units), ffn_part(ffn_w, 0)],
        out_specs=[full(rows, d)] + [full(rows, units)] * 2,
        out_shape=[jax.ShapeDtypeStruct((rows, d), BF16)]
        + [jax.ShapeDtypeStruct((rows, units), BF16)] * 2,
        compiler_params=params(),
        cost_estimate=cost(rows * d * units * 4, rows * d * 4 + units * d * 2),
        name="fe",
    )(*pieces, grad, ffn_w)


def feed_out_kernel(a_ref, w_ref, o_ref):
    o_ref[...] = dot(a_ref[...], w_ref[0], 1, 0).astype(BF16)


def feed_out(act, ffn_w):
    rows, units = act.shape
    d = ffn_w.shape[2]
    return pl.pallas_call(
        feed_out_kernel,
        grid=(1,),
        in_specs=[full(rows, units), ffn_part(ffn_w, 1)],
        out_specs=full(rows, d),
        out_shape=jax.ShapeDtypeStruct((rows, d), BF16),
        compiler_params=params(),
        cost_estimate=cost(rows * d * units * 2, rows * d * 2 + units * d * 2),
        name="fo",
    )(act, ffn_w)


def products_kernel(counts, *refs):
    k = len(counts)
    at = k
    total = None
    for i, m in enumerate(counts):
        part = dot(refs[i][...], rows_joined(refs[at : at + m]), 0, 0)
        total = part if total is None else total + part
        at += m
    refs[at][...] = total.astype(BF16)


def sum_of_products(left, right):
    f, d = left[0].shape[1], right[0][0].shape[1]
    tile = 512
    pieces = [p for group in right for p in group]
    rows = sum(a.shape[0] for a in left)
    return pl.pallas_call(
        functools.partial(products_kernel, [len(g) for g in right]),
        grid=(d // tile,),
        in_specs=[full(*a.shape) for a in left]
        + [pl.BlockSpec((p.shape[0], tile), lambda i: (0, i)) for p in pieces],
        out_specs=pl.BlockSpec((f, tile), lambda i: (0, i)),
        out_shape=jax.ShapeDtypeStruct((f, d), BF16),
        compiler_params=params(),
        cost_estimate=cost(rows * f * d * 2, rows * (f + d) * 2 + f * d * 2),
        name="sp",
    )(*left, *pieces)


def place_kernel(spots, turned, ids, *refs):
    o_ref = refs[-1]
    for (j, at, rows), ref in zip(spots, refs):
        to = block_at(ids, j, rows)
        block = ref[at : at + rows, :].astype(F32)
        if turned:
            o_ref[:, to] = block.T
        else:
            o_ref[to, :] = block


def place(ids, items, rows, turned):
    n = len(items)
    d = items[0][2].shape[1]
    in_kernel = turned and rows % 128 == 0
    shape = (d, n * rows) if in_kernel else (n * rows, d)
    out = pl.pallas_call(
        functools.partial(place_kernel, [(j, at, rows) for j, at, _ in items], in_kernel),
        grid_spec=pltpu.PrefetchScalarGridSpec(
            num_scalar_prefetch=1,
            grid=(1,),
            in_specs=[fixed_spec(*p.shape) for _, _, p in items],
            out_specs=fixed_spec(*shape),
        ),
        out_shape=jax.ShapeDtypeStruct(shape, F32),
        compiler_params=params(),
        cost_estimate=cost(0, n * rows * d * 6),
        name="pr",
    )(ids, *[p for _, _, p in items])
    return out.T if turned and not in_kernel else out


def entering(own, lg, rows, per_seq, me, backward, hold):
    if per_seq == 1:
        return jnp.zeros_like(own)
    core = lax.bitwise_and(me, 1)
    last = core == (0 if backward else 1)
    low = own.astype(BF16)
    sibling = swap(low, 1).astype(F32)
    step = jnp.exp(rows * lg)[:, None, None]
    held = after(lg, hold)
    if per_seq == 2:
        return jnp.where(last, sibling, 0.0)
    total = jnp.where(last, own + step * sibling, step * own + sibling).astype(BF16)
    size = KEY_DIM // 2
    part = lax.dynamic_slice_in_dim(total, core * size, size, 1)
    chip = me // 2
    state = jnp.zeros(part.shape, F32)
    for j in range(1, per_seq // 2):
        other = lax.bitwise_xor(chip, j)
        gap = (other - chip) if backward else (chip - other)
        scale = jnp.exp(2.0 * rows * jnp.maximum(gap - 1, 0).astype(F32) * held)
        scale = jnp.where(gap > 0, scale, 0.0)[:, None, None]
        got = swap(part, 2 * j)
        state = state + scale * got.astype(F32)
    state = state.astype(BF16)
    other = swap(state, 1)
    low_half = jnp.where(core == 0, state, other)
    high_half = jnp.where(core == 0, other, state)
    state = jnp.concatenate([low_half, high_half], axis=1).astype(F32)
    return jnp.where(last, step * state + sibling, state)


def row_dots(left, right, at):
    total, row = 0.0, 0
    for r in right:
        total = total + dot(left[row : row + r.shape[0], at], r, 0, 0)
        row += r.shape[0]
    return total


def column_dots(left, right, at):
    return sum(dot(r[:, at], a, 0, 0) for a, r in zip(left, right))


def layer(
    layer_input,
    gain_one,
    query_weight,
    key_weight,
    value_weight,
    gate_weight,
    out_weight,
    gain_two,
    up_weight,
    down_weight,
    cotangent,
):
    rows, d_part = layer_input.shape
    n_seq = lax.axis_size("seq")
    n_tp = lax.axis_size("tp")
    d = d_part * n_tp
    me = lax.axis_index("seq").astype(jnp.int32)
    t = lax.axis_index("tp").astype(jnp.int32)
    ids = jnp.stack([me, t])
    heads = query_weight.shape[1] // KEY_DIM
    seq_length = min(MAXLEN, rows * n_seq)
    per_seq = max(seq_length // rows, 1)

    blocks = rows // BLOCK
    own_half = BLOCK // n_tp

    x_full = lax.all_gather(layer_input, "tp", axis=1, tiled=True)
    half_out = out_weight.shape[0] // 2
    w_a = jnp.concatenate([query_weight, value_weight, out_weight[:half_out].T], axis=1)
    w_b = jnp.concatenate([key_weight, gate_weight, out_weight[half_out:].T], axis=1)
    w_a = xor_gather(w_a, False)
    w_b = xor_gather(w_b, True)
    w_a = [w_a[j] for j in range(n_seq)]
    w_b = [w_b[j] for j in range(n_seq)]

    gains = {0: jnp.stack([gain_one, gain_two])}
    bit = 1
    while bit < n_tp:
        for j in list(gains):
            gains[j ^ bit] = swap(gains[j], bit, "tp")
        bit *= 2
    gains = jnp.stack([gains[j] for j in range(n_tp)])[lax.bitwise_xor(t, jnp.arange(n_tp))]
    gains = gains.transpose(1, 0, 2).reshape(2, d)
    gain_one_full, gain_two_full = gains[0:1], gains[1:2]

    units = up_weight.shape[1] // n_seq
    ffn_own = jnp.stack(
        [
            lax.dynamic_slice_in_dim(up_weight, me * units, units, 1).T,
            lax.dynamic_slice_in_dim(down_weight, me * units, units, 0),
        ]
    )
    ffn_w = lax.all_gather(ffn_own, "tp", axis=1, tiled=True)

    cot_from = cotangent.reshape(blocks, n_tp, own_half, d_part)
    cot_rows = jnp.zeros((blocks, own_half, d), BF16)
    for j in range(n_tp):
        to = lax.bitwise_xor(t, j)
        block = lax.dynamic_index_in_dim(cot_from, to, 1, False)
        if j:
            block = swap(block, j, "tp")
        cot_rows = lax.dynamic_update_slice_in_dim(cot_rows, block, to * d_part, 2)
    cots = [plane_gather(cot_rows[i]) for i in range(blocks)]
    head_ids = t * heads + jnp.arange(heads)
    lg = jnp.log(1.0 - jnp.exp2(-5.0 - head_ids.astype(F32)))
    first = (me * rows) % seq_length
    half_key = KEY_DIM // 2
    freq = jnp.exp(-math.log(10000.0) * jnp.arange(half_key, dtype=F32) / half_key)
    angles = (first + jnp.arange(rows)).astype(F32)[:, None] * freq[None, :]
    cos, sin = jnp.cos(angles), jnp.sin(angles)

    shared, key, value, own_end = key_value(ids, lg, after(x_full, ffn_own), gain_one_full, cos, sin, w_a, w_b)
    query, gate = query_gate(ids, shared, cos, sin, w_a, w_b, heads)
    state_in = entering(own_end, lg, rows, per_seq, me, False, query)
    retained, mixed, branch = retain(ids, lg, query, key, value, gate, state_in, w_a, w_b, d)
    for i in range(blocks):
        branch[i] = lax.psum_scatter(branch[i], "tp", scatter_dimension=0, tiled=True)

    grad_acts = []
    for i in range(blocks):
        grad_acts.append([grad_act(p, ffn_w) for p in cots[i]])

    hidden, fed, gathered, grad_hidden, grad_branch, gain_two_part = [], [], [], [], [], 0.0
    holds = []
    for i in range(blocks):
        h, nrm = norm_two(ids, branch[i], x_full, gain_two_full, i, n_tp)
        hidden.append(h)
        gathered.append(plane_gather(nrm))
        fed.append([feed(gathered[i][k], grad_acts[i][k], ffn_w) for k in range(2)])
        grad_two = plane_reduce(fed[i][0][0], fed[i][1][0])
        gh, br, gg = norm_two_back(ids, grad_two, h, cot_rows[i], gain_two_full, n_seq)
        grad_hidden.append(gh)
        gain_two_part = gain_two_part + gg
        grad_branch.append(lax.all_gather(br, "tp", axis=0, tiled=True))
        holds.append(br)
    hold = holds[-1]

    outs = [
        [feed_out(after(fed[i][k][1], holds[i]), ffn_w) for k in range(2)] for i in range(blocks)
    ]
    quarters = [(i, k) for i in range(blocks) for k in range(2)]
    up_grad = sum_of_products(
        [after(fed[i][k][2], hold) for i, k in quarters], [gathered[i][k] for i, k in quarters]
    )
    down_grad = sum_of_products(
        [after(fed[i][k][1], hold) for i, k in quarters], [cots[i][k] for i, k in quarters]
    )
    up_grad = lax.psum_scatter(up_grad, "tp", scatter_dimension=0, tiled=True)
    down_grad = lax.psum_scatter(down_grad, "tp", scatter_dimension=0, tiled=True)

    grad_gate, grad_ret, own_first = [], [], 0.0
    for i in range(blocks):
        gg, gr, part = gate_back(
            ids, lg, grad_branch[i], query, gate, retained[i], w_a, w_b, i
        )
        grad_gate.append(gg)
        grad_ret.append(gr)
        own_first = own_first + part
    sent_g = row_dots(shared, grad_gate, slice(d // 2, d)).astype(BF16)
    sent_o = column_dots(mixed, grad_branch, slice(d // 2, d)).astype(BF16)
    kept_g = row_dots(shared, grad_gate, slice(0, d // 2))
    kept_o = column_dots(mixed, grad_branch, slice(0, d // 2))
    grad_end = entering(own_first, lg, rows, per_seq, me, True, sent_o)
    gate_grad = plane_reduce(kept_g, sent_g)
    out_grad = plane_reduce(kept_o, sent_o).T

    dqkv = retain_back(lg, query, key, value, grad_ret, state_in, grad_end, cos, sin)
    held, gain_one_part = input_back(
        ids, dqkv, grad_gate, x_full, gain_one_full, grad_hidden, w_a, w_b
    )
    input_grad = lax.psum_scatter(held, "tp", scatter_dimension=1, tiled=True)

    dqkv = after(dqkv, held)
    sent = dot(shared[:, d // 2 :], dqkv, 0, 0).astype(BF16)
    kept = dot(shared[:, : d // 2], dqkv, 0, 0)
    total = chip_sum(kept, sent)
    qkv_grad = plane_sum(total)
    kq = heads * KEY_DIM
    query_grad, key_grad, value_grad = jnp.split(qkv_grad, [kq, 2 * kq], axis=1)

    ffn = [hidden[i] + plane_reduce(outs[i][0], outs[i][1], total) for i in range(blocks)]
    out_rows = jnp.stack(ffn).astype(BF16)
    layer_output = after(jnp.zeros((blocks, n_tp, own_half, d_part), BF16), total)
    for j in range(n_tp):
        to = lax.bitwise_xor(t, j)
        block = lax.dynamic_slice_in_dim(out_rows, to * d_part, d_part, 2)
        if j:
            block = swap(block, j, "tp")
        layer_output = lax.dynamic_update_slice_in_dim(layer_output, block[:, None], to, 1)
    layer_output = layer_output.reshape(rows, d_part)

    placed = []
    for turned, part in ((True, up_grad), (False, down_grad)):
        groups = plane_gather(part)
        items = [(2 * i + c, 0, p) for c, group in enumerate(groups) for i, p in enumerate(group)]
        placed.append(place(ids, items, units, turned))
    up_grad, down_grad = placed

    sums = jnp.concatenate([gain_one_part, gain_two_part], axis=0)
    for axis, n in (("tp", n_tp), ("seq", n_seq)):
        bit = 1
        while bit < n:
            sums = sums + swap(sums, bit, axis)
            bit *= 2
    sums = lax.dynamic_slice_in_dim(sums, t * d_part, d_part, 1)

    return (
        layer_output,
        input_grad,
        sums[0],
        query_grad,
        key_grad,
        value_grad,
        gate_grad,
        out_grad,
        sums[1],
        up_grad,
        down_grad,
    )


def solution(mesh):
    placed = (
        P("seq", "tp"),
        P("tp"),
        P("seq", "tp"),
        P("seq", "tp"),
        P("seq", "tp"),
        P("seq", "tp"),
        P("tp", "seq"),
        P("tp"),
        P(None, "tp"),
        P("tp", None),
        P("seq", "tp"),
    )
    return jax.shard_map(
        layer,
        mesh=mesh,
        in_specs=placed,
        out_specs=(
            P("seq", "tp"),
            P("seq", "tp"),
            P("tp"),
            P("seq", "tp"),
            P("seq", "tp"),
            P("seq", "tp"),
            P("seq", "tp"),
            P("tp", "seq"),
            P("tp"),
            P(None, "tp"),
            P("tp", None),
        ),
        check_vma=False,
    )
```
